32 devices in a mesh: grp: 2 (over y), ep: 4 (over z), tp: 2 (over x), mb: 2 (over core).
Axes of the slice: x: 2, y: 2, z: 4, core: 2. Of those that a mesh axis runs over, the one named last changes fastest.
Arguments:
- hidden: bfloat16 [256, 3584], P(('grp', 'ep', 'mb'), 'tp'), parts along dimension 0, may hold values from -12 to 12
- moe_gain: float32 [3584], P('tp'), may hold values from 0.1 to 1.9
- expert_ids: int32 [256, 8], P(('grp', 'ep', 'mb')), parts along dimension 0, may hold values from 0 to 7, as said below
- slots: int32 [256, 8], P(('grp', 'ep', 'mb')), parts along dimension 0, may hold values from 0 to 15, as said below
- affinity: float32 [256, 8], P(('grp', 'ep', 'mb')), parts along dimension 0, may hold values from 0.05 to 1
- w_gate: bfloat16 [8, 3584, 1024], P(('ep', 'mb'), None, 'tp'), may hold values from -0.09375 to 0.09375
- w_up: bfloat16 [8, 3584, 1024], P(('ep', 'mb'), None, 'tp'), may hold values from -0.09375 to 0.09375
- w_down: bfloat16 [8, 1024, 3584], P(('ep', 'mb'), 'tp'), may hold values from -0.1875 to 0.1875
- attn_gain: float32 [3584], P('tp'), may hold values from 0.1 to 1.9
- w_dkv: bfloat16 [3584, 576], P('tp'), may hold values from -0.09375 to 0.09375
- kv_gain: float32 [512], replicated, may hold values from 0.1 to 1.9
- queries: bfloat16 [256, 64, 576], P(('grp', 'ep', 'mb'), 'tp'), parts along dimension 0, may hold values from -36 to 36
- cache: bfloat16 [256, 128, 576], P(('grp', 'ep', 'mb'), 'tp'), parts along dimension 0, may hold values from -4 to 4
- lengths: int32 [256], P(('grp', 'ep', 'mb')), parts along dimension 0, may hold values from 2 to 128
Outputs:
- next_hidden: bfloat16 [256, 3584], P(('grp', 'ep', 'mb'), 'tp'), parts along dimension 0
- latent_out: bfloat16 [256, 64, 512], P(('grp', 'ep', 'mb'), 'tp'), parts along dimension 0
The draws below stay inside these ranges and needn't reach their ends.
There are 2 independent parts, one for each index of `grp`. The reference program is written for one: setup_inputs(seed, part) draws one part's arguments, and reference() takes and returns one part's arrays. A program takes and returns all parts, laid end to end along the dimension named above; an argument that names none is the same for every part. Nothing has to cross between parts.
Inputs may be any that keep to these rules, and one draw needn't show every extreme that they name: `expert_ids`: each row names 8 different experts; in every draw some expert is named by every token. slots[t, k] is the rank of the choice (t, k) among the choices of the same expert made by the 16 tokens of one device; these ranks are distinct and run from 0 upward. A choice whose slot is 8 or more is dropped.
All inputs are finite; a program needn't handle non-finite values.
Results may differ from the reference program's by a relative error of at most 0.017.
Values may be sent and summed in bfloat16 or wider, within the bound.
A program may use at most 128 MiB of HBM per device.

```python
import math
import jax
import jax.numpy as jnp
from jax import lax

D = 3584
H = 1024
HEADS = 64
LAT = 512
KVC = 576
TOP = 8
TOK_DEV = 16
KV = 128
CAP = 8
EXPERTS = 8
TOKENS = 128
N_TP = 2


def routing(key):
    base_key = jax.random.fold_in(key, 7)
    hot_expert = jax.random.randint(jax.random.fold_in(base_key, 1), (), 0, EXPERTS)
    expert_iota = jnp.arange(EXPERTS, dtype=jnp.int32)
    biases = jax.random.randint(jax.random.fold_in(base_key, 2), (EXPERTS,), 0, 4 * EXPERTS)
    biases = jnp.where(expert_iota == hot_expert, 16 * EXPERTS, biases)
    noise_int = jax.random.randint(jax.random.fold_in(base_key, 3), (TOKENS, EXPERTS), 0, 6 * EXPERTS)
    scores = (noise_int + biases[None, :]) * EXPERTS + expert_iota[None, :]
    chosen = lax.top_k(scores, TOP)[1].astype(jnp.int32)
    priority = jax.random.randint(jax.random.fold_in(base_key, 4), (TOKENS, TOP), 0, 4096) * (TOKENS * TOP)
    priority = priority + jnp.arange(TOKENS * TOP, dtype=jnp.int32).reshape(TOKENS, TOP)
    blocks = TOKENS // TOK_DEV
    block_ids = chosen.reshape(blocks, TOK_DEV * TOP)
    block_prio = priority.reshape(blocks, TOK_DEV * TOP)
    same_expert = block_ids[:, :, None] == block_ids[:, None, :]
    earlier = block_prio[:, None, :] < block_prio[:, :, None]
    ranks = jnp.sum((same_expert & earlier).astype(jnp.int32), -1)
    return (chosen, ranks.reshape(TOKENS, TOP).astype(jnp.int32))


def draw_expert_ids(key, part):
    return routing(key)[0]


def draw_slots(key, part):
    return routing(key)[1]


def cache_normal(key):
    return jnp.clip(jax.random.normal(jax.random.fold_in(key, 31), (TOKENS, KV, KVC), jnp.float32), -4.0, 4.0)


def draw_cache(key, part):
    values = cache_normal(key)
    return values.astype(jnp.bfloat16)


def draw_queries(key, part):
    values = jnp.clip(jax.random.normal(jax.random.fold_in(key, 34), (TOKENS, HEADS, KVC), jnp.float32), -4.0, 4.0)
    return values.astype(jnp.bfloat16)


def draw_hidden(key, part):
    column_scale = 0.6 + 1.2 * jnp.arange(D, dtype=jnp.float32) / D
    values = jnp.clip(jax.random.normal(jax.random.fold_in(key, 44), (TOKENS, D), jnp.float32), -4.0, 4.0) * column_scale[None, :]
    return jnp.clip(values, -12.0, 12.0).astype(jnp.bfloat16)


def set_ends(result, rng, smallest, top_value):
    dims = result.shape
    place = [jax.random.randint(jax.random.fold_in(rng, axis), (), 0, dims[axis]) for axis in range(len(dims))]
    result = result.at[tuple(place)].set(smallest)
    longest = dims.index(max(dims))
    place[longest] = (place[longest] + 1) % dims[longest]
    return result.at[tuple(place)].set(top_value)


def block_levels(key, shape, cuts, smallest, largest):
    level = 1.0
    for dim, parts in cuts:
        draws = jax.random.uniform(jax.random.fold_in(jax.random.fold_in(key, 6), dim), (parts,), jnp.float32, smallest / len(cuts), largest / len(cuts))
        level = level * jnp.repeat(jnp.exp(draws), shape[dim] // parts).reshape((-1,) + (1,) * (len(shape) - 1 - dim))
    return level


def centred(own_key, dims, spread, limit, cuts=(), kind=jnp.bfloat16):
    loudness = block_levels(own_key, dims, cuts, -0.22, 0.18) if cuts else 1.0
    array = jax.random.normal(own_key, dims, jnp.float32) * spread * loudness
    return jnp.minimum(jnp.maximum(array, -limit), limit).astype(kind)


def setup_inputs(seed: int = 0, part: int = 0) -> dict:
    splits = jax.random.split(jax.random.key(seed), 15)
    part_keys = jax.random.split(jax.random.fold_in(splits[14], part), 15)
    hidden = draw_hidden(jax.random.fold_in(jax.random.fold_in(splits[14], part), 71), part)
    moe_gain = jnp.clip(1.0 + 0.18 * jax.random.normal(splits[1], (D,), jnp.float32), 0.1, 1.9)
    expert_ids = draw_expert_ids(jax.random.fold_in(jax.random.fold_in(splits[14], part), 71), part)
    slots = draw_slots(jax.random.fold_in(jax.random.fold_in(splits[14], part), 71), part)
    affinity = jnp.clip(jnp.exp(math.log(1.0) - 2.9957323 * jax.random.uniform(part_keys[4], (TOKENS, TOP), jnp.float32) ** block_levels(part_keys[4], (TOKENS, TOP), ((0, 8),), -0.2, 0.2)), 0.05, 1.0)
    w_gate = centred(splits[5], (EXPERTS, D, H), D ** -0.5, 0.09375, ((0, 8), (2, 2)))
    w_up = centred(splits[6], (EXPERTS, D, H), D ** -0.5, 0.09375, ((0, 8), (2, 2)))
    w_down = centred(splits[7], (EXPERTS, H, D), H ** -0.5, 0.1875, ((0, 8), (1, 2)))
    attn_gain = jnp.clip(1.0 + 0.18 * jax.random.normal(splits[8], (D,), jnp.float32), 0.1, 1.9)
    w_dkv = centred(splits[9], (D, KVC), D ** -0.5, 0.09375, ((0, 2),))
    kv_gain = jnp.clip(1.0 + 0.18 * jax.random.normal(splits[10], (LAT,), jnp.float32), 0.1, 1.9)
    queries = draw_queries(jax.random.fold_in(jax.random.fold_in(splits[14], part), 71), part)
    cache = draw_cache(jax.random.fold_in(jax.random.fold_in(splits[14], part), 71), part)
    lengths = set_ends(jax.random.randint(part_keys[13], (TOKENS,), 2, KV + 1), jax.random.fold_in(part_keys[13], 1), 2, KV).astype(jnp.int32)
    return dict(hidden=hidden, moe_gain=moe_gain, expert_ids=expert_ids, slots=slots, affinity=affinity, w_gate=w_gate, w_up=w_up, w_down=w_down, attn_gain=attn_gain, w_dkv=w_dkv, kv_gain=kv_gain, queries=queries, cache=cache, lengths=lengths)


epsilon = 1e-06
route_scale = 2.5
score_scale = 192.0 ** (-0.5)

def root_norm(values, gain):
    return values * lax.rsqrt(lax.optimization_barrier(jnp.mean(values * values, -1, keepdims=True)) + epsilon) * gain

def rope_rotate(rope_part, position):
    half_rope = rope_part.shape[-1] // 2
    inv_freq = 10000.0 ** (-jnp.arange(half_rope, dtype=jnp.float32) / half_rope)
    angles = position[:, None] * inv_freq[None, :]
    cos_table = jnp.cos(angles)
    sin_table = jnp.sin(angles)
    first_half = rope_part[:, :half_rope]
    second_half = rope_part[:, half_rope:]
    return jnp.concatenate([first_half * cos_table - second_half * sin_table, first_half * sin_table + second_half * cos_table], 1)

def reference(hidden, moe_gain, expert_ids, slots, affinity, w_gate, w_up, w_down, attn_gain, w_dkv, kv_gain, queries, cache, lengths):
    hidden_wide = hidden.astype(jnp.float32)
    normed = root_norm(hidden_wide, moe_gain).astype(jnp.bfloat16)
    kept_rows = slots < CAP
    weight = route_scale * affinity / lax.optimization_barrier(jnp.sum(affinity, -1, keepdims=True)) * kept_rows.astype(jnp.float32)
    source = (jnp.arange(TOKENS, dtype=jnp.int32) // TOK_DEV)[:, None]
    flat_slot = ((expert_ids * EXPERTS + source) * CAP + jnp.minimum(slots, CAP - 1)).astype(jnp.int32)
    slot_count = EXPERTS * EXPERTS * CAP
    token_iota = jnp.broadcast_to(jnp.arange(TOKENS, dtype=jnp.int32)[:, None], (TOKENS, TOP))
    target = jnp.where(kept_rows, flat_slot, slot_count).astype(jnp.int32)
    token_of = jnp.full((slot_count,), TOKENS, jnp.int32).at[target].set(token_iota, mode='drop')
    padded = jnp.concatenate([normed, jnp.zeros((1, D), jnp.bfloat16)], 0)
    expert_rows = padded[token_of].reshape(EXPERTS, EXPERTS * CAP, D)

    def expert_block(operands):
        rows_in, gate_weight, up_weight, down_weight = operands
        gate_act = jnp.dot(rows_in, gate_weight, preferred_element_type=jnp.float32)
        up_act = jnp.dot(rows_in, up_weight, preferred_element_type=jnp.float32)
        units = (jax.nn.silu(gate_act) * up_act).astype(jnp.bfloat16)
        grouped = units.reshape(EXPERTS * CAP, N_TP, H // N_TP).astype(jnp.float32)
        down_groups = down_weight.reshape(N_TP, H // N_TP, D).astype(jnp.float32)
        partials = jnp.einsum('rth,thd->trd', grouped, down_groups)
        return lax.optimization_barrier(jnp.sum(partials.astype(jnp.bfloat16).astype(jnp.float32), 0))
    expert_out = lax.map(expert_block, (expert_rows, w_gate, w_up, w_down)).reshape(slot_count, D)
    picked = expert_out[jnp.where(kept_rows, flat_slot, 0).astype(jnp.int32)]
    moe_out = lax.optimization_barrier(jnp.sum(picked * weight[:, :, None], 1))
    next_hidden = (hidden_wide + moe_out).astype(jnp.bfloat16)
    normed_attn = root_norm(next_hidden.astype(jnp.float32), attn_gain).astype(jnp.bfloat16)
    down_kv = jnp.dot(normed_attn, w_dkv, preferred_element_type=jnp.float32)
    latent_part = root_norm(down_kv[:, :LAT], kv_gain)
    rope_part = rope_rotate(down_kv[:, LAT:], lengths.astype(jnp.float32))
    new_key = jnp.concatenate([latent_part, rope_part], 1).astype(jnp.bfloat16)
    query_wide = queries.astype(jnp.float32)
    cache_wide = cache.astype(jnp.float32)
    scores = jnp.einsum('bhc,bjc->bhj', query_wide, cache_wide) * score_scale
    live_mask = (jnp.arange(KV, dtype=jnp.int32)[None, :] < lengths[:, None])[:, None, :]
    scores = jnp.where(live_mask, scores, -1e+30)
    own_score = jnp.einsum('bhc,bc->bh', query_wide, new_key.astype(jnp.float32)) * score_scale
    peak_all = jnp.maximum(lax.optimization_barrier(jnp.max(scores, -1)), own_score)
    prob_live = jnp.where(live_mask, jnp.exp(scores - peak_all[:, :, None]), 0.0)
    own_prob = jnp.exp(own_score - peak_all)
    mass_total = lax.optimization_barrier(jnp.sum(prob_live, -1)) + own_prob
    numerator = jnp.einsum('bhj,bjc->bhc', prob_live.astype(jnp.bfloat16).astype(jnp.float32), cache_wide[:, :, :LAT])
    numerator = numerator + own_prob.astype(jnp.bfloat16).astype(jnp.float32)[:, :, None] * new_key[:, None, :LAT].astype(jnp.float32)
    latent_out = (numerator / mass_total[:, :, None]).astype(jnp.bfloat16)
    return (next_hidden, latent_out)
```

```python
import functools

import jax
import jax.numpy as jnp
from jax import lax
from jax.experimental import pallas as pl
from jax.experimental.pallas import tpu as pltpu
from jax.sharding import PartitionSpec as P

CAP = 8
GROUPS = 4
epsilon = 1e-06
route_scale = 2.5
score_scale = 192.0 ** (-0.5)
MESH = pl.DeviceIdType.MESH
F32 = jnp.float32
BF16 = jnp.bfloat16


def up(value, step):
    return -(-value // step) * step


def kernel(
    n_tp,
    n_ep,
    n_mb,
    hidden,
    moe_gain,
    ids,
    slots,
    affinity,
    w_gate,
    w_up,
    w_down,
    attn_gain,
    w_dkv,
    kv_gain,
    queries,
    cache,
    lengths,
    next_out,
    latent_out,
    hid_all,
    gain_all,
    send,
    arrived,
    wg,
    wu,
    wd,
    wk,
    ret_send,
    ret,
    tsum,
    rs_send,
    rs_recv,
    key_send,
    key_recv,
    q_buf,
    kv_buf,
    acc,
    peaks,
    masses,
    keys,
    load_sem,
    kv_load_sem,
    hid_ssem,
    hid_rsem,
    gain_ssem,
    gain_rsem,
    kv_ssem,
    kv_rsem,
    row_ssem,
    row_rsem,
    ret_ssem,
    ret_rsem,
    rs_ssem,
    rs_rsem,
    key_ssem,
    key_rsem,
):
    experts = n_ep * n_mb
    tokens, d_loc = hidden.shape
    d_all = d_loc * n_tp
    lat = kv_gain.shape[1]
    kvc = cache.shape[2]
    per_group = tokens // GROUPS
    tp = lax.axis_index("tp")
    me = lax.axis_index("ep") * n_mb + lax.axis_index("mb")

    def tp_id(step):
        return lax.rem(tp + step, n_tp)

    def ex_id(step):
        return lax.rem(me + step, experts)

    def ex_dev(index):
        return {"ep": index // n_mb, "mb": lax.rem(index, n_mb)}

    local = [
        pltpu.make_async_copy(hidden, hid_all.at[tp], load_sem.at[0]),
        pltpu.make_async_copy(moe_gain, gain_all.at[tp], load_sem.at[1]),
        pltpu.make_async_copy(queries, q_buf, load_sem.at[2]),
        pltpu.make_async_copy(w_gate.at[0], wg, load_sem.at[3]),
        pltpu.make_async_copy(w_up.at[0], wu, load_sem.at[4]),
        pltpu.make_async_copy(w_down.at[0], wd, load_sem.at[5]),
        pltpu.make_async_copy(w_dkv, wk, load_sem.at[6]),
    ]
    kv_load = pltpu.make_async_copy(cache, kv_buf.at[:, tp], kv_load_sem)
    local[0].start()
    local[1].start()

    barrier = pltpu.get_barrier_semaphore()
    for step in range(1, n_tp):
        pl.semaphore_signal(barrier, inc=1, device_id={"tp": tp_id(step)}, device_id_type=MESH)
    for step in range(1, experts):
        pl.semaphore_signal(barrier, inc=1, device_id=ex_dev(ex_id(step)), device_id_type=MESH)
    pl.semaphore_wait(barrier, n_tp - 1 + experts - 1)

    def tp_copy(src, dst, ssem, rsem, step):
        return pltpu.make_async_remote_copy(
            src_ref=src,
            dst_ref=dst,
            send_sem=ssem,
            recv_sem=rsem,
            device_id={"tp": tp_id(step)},
            device_id_type=MESH,
        )

    def arrival(dst, rsem):
        return pltpu.make_async_copy(dst, dst, rsem)

    sends = []
    for step in range(1, n_tp):
        for src, dst, ssem, rsem in (
            (hidden, hid_all, hid_ssem, hid_rsem),
            (moe_gain, gain_all, gain_ssem, gain_rsem),
        ):
            copy = tp_copy(src, dst.at[tp], ssem.at[step], rsem.at[tp], step)
            copy.start()
            sends.append(copy)
    for copy in local[2:5]:
        copy.start()
    kv_load.start()
    for copy in local[5:]:
        copy.start()

    kept = slots[...] < CAP
    aff = affinity[...]
    weight = route_scale * aff / jnp.sum(aff, -1, keepdims=True) * kept.astype(F32)
    target = jnp.where(kept, ids[...] * CAP + slots[...], -1)
    rows = experts * CAP
    iota = lax.broadcasted_iota(jnp.int32, (tokens, rows), 1)
    dispatch = jnp.zeros((tokens, rows), F32)
    combine = jnp.zeros((tokens, rows), F32)
    for k in range(ids.shape[1]):
        match = target[:, k : k + 1] == iota
        dispatch = jnp.where(match, 1.0, dispatch)
        combine = jnp.where(match, weight[:, k : k + 1], combine)
    dispatch = dispatch.T.astype(BF16)
    high = combine.astype(BF16)
    rest = combine - high.astype(F32)
    mid = rest.astype(BF16)
    low = (rest - mid.astype(F32)).astype(BF16)
    combine3 = jnp.concatenate([high, mid, low], 0)

    local[0].wait()
    local[1].wait()
    for step in range(1, n_tp):
        arrival(hid_all.at[tp_id(step)], hid_rsem.at[tp_id(step)]).wait()
        arrival(gain_all.at[tp_id(step)], gain_rsem.at[tp_id(step)]).wait()
    square = jnp.zeros((tokens, 1), F32)
    for b in range(n_tp):
        wide = hid_all[b].astype(F32)
        square = square + jnp.sum(wide * wide, -1, keepdims=True)
    scale = lax.rsqrt(square / d_all + epsilon)
    for b in range(n_tp):
        normed = (hid_all[b].astype(F32) * scale * gain_all[b]).astype(BF16)
        picked = jnp.dot(dispatch, normed, preferred_element_type=F32)
        send[:, b] = picked.reshape(experts, CAP, d_loc).astype(BF16)
    for step in range(1, experts):
        peer = ex_id(step)
        copy = pltpu.make_async_remote_copy(
            src_ref=send.at[peer],
            dst_ref=arrived.at[me],
            send_sem=row_ssem.at[step],
            recv_sem=row_rsem.at[me],
            device_id=ex_dev(peer),
            device_id_type=MESH,
        )
        copy.start()
        sends.append(copy)
    for g in range(GROUPS):
        span = pl.ds(g * per_group, per_group)
        for step in range(1, n_tp):
            copy = tp_copy(
                cache.at[span], kv_buf.at[span, tp], kv_ssem.at[step, g], kv_rsem.at[tp, g], step
            )
            copy.start()
            sends.append(copy)
    arrived[me] = send[me]

    local[2].wait()
    kv_load.wait()
    heads = queries.shape[1]
    span_len = cache.shape[1]
    total_len = n_tp * span_len

    def attend(g):
        span = pl.ds(g * per_group, per_group)
        for step in range(1, n_tp):
            arrival(kv_buf.at[span, tp_id(step)], kv_rsem.at[tp_id(step), g]).wait()

        def body(i, carry):
            t = g * per_group + i
            block = kv_buf[t].reshape(total_len, kvc)
            scores = (
                lax.dot_general(
                    q_buf[t], block, (((1,), (1,)), ((), ())), preferred_element_type=F32
                )
                * score_scale
            )
            live = lax.broadcasted_iota(jnp.int32, (heads, total_len), 1) < lengths[t]
            scores = jnp.where(live, scores, -1e30)
            peak = jnp.max(scores, -1, keepdims=True)
            prob = jnp.where(live, jnp.exp(scores - peak), 0.0)
            mass = jnp.sum(prob, -1, keepdims=True)
            acc[t] = jnp.dot(prob.astype(BF16), block[:, :lat], preferred_element_type=F32)
            peaks[t] = jnp.broadcast_to(peak, (heads, 128))
            masses[t] = jnp.broadcast_to(mass, (heads, 128))
            return carry

        lax.fori_loop(0, per_group, body, 0)

    attend(0)

    for step in range(1, experts):
        arrival(arrived.at[ex_id(step)], row_rsem.at[ex_id(step)]).wait()
    local[3].wait()
    local[4].wait()
    gate = jnp.zeros((rows, wg.shape[1]), F32)
    upper = jnp.zeros((rows, wg.shape[1]), F32)
    for b in range(n_tp):
        block = arrived[:, b].astype(F32).reshape(rows, d_loc).astype(BF16)
        gate = gate + jnp.dot(block, wg[b * d_loc : (b + 1) * d_loc], preferred_element_type=F32)
        upper = upper + jnp.dot(block, wu[b * d_loc : (b + 1) * d_loc], preferred_element_type=F32)
    units = (gate / (1.0 + jnp.exp(-gate)) * upper).astype(BF16)
    local[5].wait()
    width = 512 if d_all % 512 == 0 else 128
    for c in range(0, d_all, width):
        part = jnp.dot(units, wd[:, c : c + width], preferred_element_type=F32)
        ret_send[:, :, c : c + width] = part.reshape(experts, CAP, width).astype(BF16)
    for step in range(1, experts):
        peer = ex_id(step)
        copy = pltpu.make_async_remote_copy(
            src_ref=ret_send.at[peer],
            dst_ref=ret.at[me],
            send_sem=ret_ssem.at[step],
            recv_sem=ret_rsem.at[me],
            device_id=ex_dev(peer),
            device_id_type=MESH,
        )
        copy.start()
        sends.append(copy)
    ret[me] = ret_send[me]
    for g in range(1, GROUPS):
        attend(g)

    for step in range(1, experts):
        arrival(ret.at[ex_id(step)], ret_rsem.at[ex_id(step)]).wait()
    for c in range(0, d_all, width):
        block = ret[:, :, c : c + width].astype(F32).reshape(rows, width).astype(BF16)
        part = jnp.dot(combine3, block, preferred_element_type=F32)
        tsum[:, c : c + width] = part[:tokens] + (
            part[tokens : 2 * tokens] + part[2 * tokens : 3 * tokens]
        )
    for p in range(n_tp):
        rs_send[p] = tsum[:, p * d_loc : (p + 1) * d_loc].astype(BF16)
    for step in range(1, n_tp):
        copy = tp_copy(
            rs_send.at[tp_id(step)], rs_recv.at[tp], rs_ssem.at[step], rs_rsem.at[tp], step
        )
        copy.start()
        sends.append(copy)
    rs_recv[tp] = rs_send[tp]
    local[6].wait()
    for step in range(1, n_tp):
        arrival(rs_recv.at[tp_id(step)], rs_rsem.at[tp_id(step)]).wait()
    moe = rs_recv[0].astype(F32)
    for p in range(1, n_tp):
        moe = moe + rs_recv[p].astype(F32)
    next_hidden = (hid_all[tp].astype(F32) + moe).astype(BF16)
    next_out[...] = next_hidden
    next_wide = next_hidden.astype(F32)
    square = jnp.sum(next_wide * next_wide, -1, keepdims=True)
    scaled = (next_wide * attn_gain[...]).astype(BF16)
    kvp = up(kvc, 128)
    if kvp > kvc:
        key_send[:, kvp - 128 : kvp] = jnp.zeros((tokens, 128), F32)
    key_send[:, :kvc] = jnp.dot(scaled, wk[...], preferred_element_type=F32)
    key_send[:, kvp : kvp + 128] = jnp.broadcast_to(square, (tokens, 128))
    for step in range(1, n_tp):
        copy = tp_copy(key_send, key_recv.at[tp], key_ssem.at[step], key_rsem.at[tp], step)
        copy.start()
        sends.append(copy)
    key_recv[tp] = key_send[...]

    half = (kvc - lat) // 2
    lane = lax.broadcasted_iota(jnp.int32, (tokens, 2 * half), 1)
    pair = jnp.where(lane < half, lane, lane - half).astype(F32)
    freq = jnp.exp(pair * (-9.210340371976184 / half))
    row_id = lax.broadcasted_iota(jnp.int32, (tokens, 2 * half), 0)
    place = jnp.zeros((tokens, 2 * half), F32)
    for t in range(tokens):
        place = jnp.where(row_id == t, lengths[t].astype(F32), place)
    angle = place * freq
    cos_table = jnp.cos(angle)
    sin_table = jnp.where(lane < half, -1.0, 1.0) * jnp.sin(angle)

    for step in range(1, n_tp):
        arrival(key_recv.at[tp_id(step)], key_rsem.at[tp_id(step)]).wait()
    total = key_recv[0]
    for p in range(1, n_tp):
        total = total + key_recv[p]
    down = total * lax.rsqrt(total[:, kvp : kvp + 1] / d_all + epsilon)
    latent = down[:, :lat]
    latent = (
        latent
        * lax.rsqrt(jnp.mean(latent * latent, -1, keepdims=True) + epsilon)
        * kv_gain[...]
    )
    rope = down[:, lat:kvc]
    swapped = jnp.concatenate([rope[:, half:], rope[:, :half]], 1)
    rope = rope * cos_table + swapped * sin_table
    keys[:, :lat] = latent.astype(BF16).astype(F32)
    keys[:, lat:kvc] = rope.astype(BF16).astype(F32)

    def finish(t, carry):
        key = keys[pl.ds(t, 1), :]
        own = jnp.sum(q_buf[t].astype(F32) * key, -1, keepdims=True) * score_scale
        peak = peaks[t][:, :1]
        mass = masses[t][:, :1]
        top = jnp.maximum(peak, own)
        factor = jnp.exp(peak - top)
        own_prob = jnp.exp(own - top)
        inverse = 1.0 / (mass * factor + own_prob)
        own_b = own_prob.astype(BF16).astype(F32)
        latent_out[t] = (acc[t] * (factor * inverse) + (own_b * inverse) * key[:, :lat]).astype(
            BF16
        )
        return carry

    lax.fori_loop(0, tokens, finish, 0)
    for copy in sends:
        copy.wait_send()


def solution(mesh):
    n_tp, n_ep, n_mb = mesh.shape["tp"], mesh.shape["ep"], mesh.shape["mb"]
    experts = n_ep * n_mb

    def local(
        hidden,
        moe_gain,
        expert_ids,
        slots,
        affinity,
        w_gate,
        w_up,
        w_down,
        attn_gain,
        w_dkv,
        kv_gain,
        queries,
        cache,
        lengths,
    ):
        tokens, d_loc = hidden.shape
        d_all = d_loc * n_tp
        heads, kvc = queries.shape[1:]
        span = cache.shape[1]
        lat = kv_gain.shape[0]
        hid_dim = w_gate.shape[2]
        wide = up(kvc, 128) + 128
        any_space = pl.BlockSpec(memory_space=pl.ANY)
        vmem = pl.BlockSpec(memory_space=pltpu.VMEM)
        smem = pl.BlockSpec(memory_space=pltpu.SMEM)
        dma = pltpu.SemaphoreType.DMA
        return pl.pallas_call(
            functools.partial(kernel, n_tp, n_ep, n_mb),
            out_shape=(
                jax.ShapeDtypeStruct((tokens, d_loc), BF16),
                jax.ShapeDtypeStruct((tokens, heads, lat), BF16),
            ),
            in_specs=[
                any_space,
                any_space,
                vmem,
                vmem,
                vmem,
                any_space,
                any_space,
                any_space,
                vmem,
                any_space,
                vmem,
                any_space,
                any_space,
                smem,
            ],
            out_specs=(vmem, vmem),
            scratch_shapes=[
                pltpu.VMEM((n_tp, tokens, d_loc), BF16),
                pltpu.VMEM((n_tp, 1, d_loc), F32),
                pltpu.VMEM((experts, n_tp, CAP, d_loc), BF16),
                pltpu.VMEM((experts, n_tp, CAP, d_loc), BF16),
                pltpu.VMEM((d_all, hid_dim), BF16),
                pltpu.VMEM((d_all, hid_dim), BF16),
                pltpu.VMEM((hid_dim, d_all), BF16),
                pltpu.VMEM((d_loc, kvc), BF16),
                pltpu.VMEM((experts, CAP, d_all), BF16),
                pltpu.VMEM((experts, CAP, d_all), BF16),
                pltpu.VMEM((tokens, d_all), F32),
                pltpu.VMEM((n_tp, tokens, d_loc), BF16),
                pltpu.VMEM((n_tp, tokens, d_loc), BF16),
                pltpu.VMEM((tokens, wide), F32),
                pltpu.VMEM((n_tp, tokens, wide), F32),
                pltpu.VMEM((tokens, heads, kvc), BF16),
                pltpu.VMEM((tokens, n_tp, span, kvc), BF16),
                pltpu.VMEM((tokens, heads, lat), F32),
                pltpu.VMEM((tokens, heads, 128), F32),
                pltpu.VMEM((tokens, heads, 128), F32),
                pltpu.VMEM((tokens, kvc), F32),
                dma((7,)),
                dma,
                dma((n_tp,)),
                dma((n_tp,)),
                dma((n_tp,)),
                dma((n_tp,)),
                dma((n_tp, GROUPS)),
                dma((n_tp, GROUPS)),
                dma((experts,)),
                dma((experts,)),
                dma((experts,)),
                dma((experts,)),
                dma((n_tp,)),
                dma((n_tp,)),
                dma((n_tp,)),
                dma((n_tp,)),
            ],
            compiler_params=pltpu.CompilerParams(
                collective_id=0, has_side_effects=True, vmem_limit_bytes=60 * 1024 * 1024
            ),
        )(
            hidden,
            moe_gain[None],
            expert_ids,
            slots,
            affinity,
            w_gate,
            w_up,
            w_down,
            attn_gain[None],
            w_dkv,
            kv_gain[None],
            queries,
            cache,
            lengths,
        )

    return jax.shard_map(
        local,
        mesh=mesh,
        in_specs=(
            P(("grp", "ep", "mb"), "tp"),
            P("tp"),
            P(("grp", "ep", "mb"), None),
            P(("grp", "ep", "mb"), None),
            P(("grp", "ep", "mb"), None),
            P(("ep", "mb"), None, "tp"),
            P(("ep", "mb"), None, "tp"),
            P(("ep", "mb"), "tp", None),
            P("tp"),
            P("tp", None),
            P(),
            P(("grp", "ep", "mb"), "tp", None),
            P(("grp", "ep", "mb"), "tp", None),
            P(("grp", "ep", "mb")),
        ),
        out_specs=(P(("grp", "ep", "mb"), "tp"), P(("grp", "ep", "mb"), "tp", None)),
        check_vma=False,
    )
```

```python
import functools

import jax
import jax.numpy as jnp
from jax import lax
from jax.experimental import pallas as pl
from jax.experimental.pallas import tpu as pltpu
from jax.sharding import PartitionSpec as P

CAP = 8
GROUPS = 4
epsilon = 1e-06
route_scale = 2.5
score_scale = 192.0 ** (-0.5)
MESH = pl.DeviceIdType.MESH
F32 = jnp.float32
BF16 = jnp.bfloat16


def up(value, step):
    return -(-value // step) * step


def kernel(
    n_tp,
    n_ep,
    n_mb,
    hidden,
    moe_gain,
    ids,
    slots,
    affinity,
    w_gate,
    w_up,
    w_down,
    attn_gain,
    w_dkv,
    kv_gain,
    queries,
    cache,
    lengths,
    next_out,
    latent_out,
    hid_all,
    gain_all,
    send,
    arrived,
    wg,
    wu,
    wd,
    wk,
    ret_send,
    ret,
    tsum,
    rs_send,
    rs_recv,
    key_send,
    key_recv,
    q_buf,
    kv_buf,
    acc,
    peaks,
    masses,
    keys,
    load_sem,
    kv_load_sem,
    hid_ssem,
    hid_rsem,
    gain_ssem,
    gain_rsem,
    kv_ssem,
    kv_rsem,
    row_ssem,
    row_rsem,
    ret_ssem,
    ret_rsem,
    rs_ssem,
    rs_rsem,
    key_ssem,
    key_rsem,
):
    experts = n_ep * n_mb
    tokens, d_loc = hidden.shape
    d_all = d_loc * n_tp
    lat = kv_gain.shape[1]
    kvc = cache.shape[2]
    per_group = tokens // GROUPS
    tp = lax.axis_index("tp")
    me = lax.axis_index("ep") * n_mb + lax.axis_index("mb")

    def tp_id(step):
        return lax.rem(tp + step, n_tp)

    def ex_id(step):
        return lax.rem(me + step, experts)

    def ex_dev(index):
        return {"ep": index // n_mb, "mb": lax.rem(index, n_mb)}

    local = [
        pltpu.make_async_copy(hidden, hid_all.at[tp], load_sem.at[0]),
        pltpu.make_async_copy(queries, q_buf, load_sem.at[1]),
        pltpu.make_async_copy(w_gate.at[0], wg, load_sem.at[2]),
        pltpu.make_async_copy(w_up.at[0], wu, load_sem.at[3]),
        pltpu.make_async_copy(w_down.at[0], wd, load_sem.at[4]),
        pltpu.make_async_copy(w_dkv, wk, load_sem.at[5]),
    ]
    kv_load = pltpu.make_async_copy(cache, kv_buf.at[:, tp], kv_load_sem)
    local[0].start()
    gain_all[tp] = moe_gain[...].reshape(1, d_loc)

    barrier = pltpu.get_barrier_semaphore()
    for step in range(1, n_tp):
        pl.semaphore_signal(barrier, inc=1, device_id={"tp": tp_id(step)}, device_id_type=MESH)
    for step in range(1, experts):
        pl.semaphore_signal(barrier, inc=1, device_id=ex_dev(ex_id(step)), device_id_type=MESH)
    pl.semaphore_wait(barrier, n_tp - 1 + experts - 1)

    def tp_copy(src, dst, ssem, rsem, step):
        return pltpu.make_async_remote_copy(
            src_ref=src,
            dst_ref=dst,
            send_sem=ssem,
            recv_sem=rsem,
            device_id={"tp": tp_id(step)},
            device_id_type=MESH,
        )

    def arrival(dst, rsem):
        return pltpu.make_async_copy(dst, dst, rsem)

    sends = []
    for step in range(1, n_tp):
        for src, dst, ssem, rsem in (
            (hidden, hid_all, hid_ssem, hid_rsem),
            (gain_all.at[tp], gain_all, gain_ssem, gain_rsem),
        ):
            copy = tp_copy(src, dst.at[tp], ssem.at[step], rsem.at[tp], step)
            copy.start()
            sends.append(copy)
    for copy in local[1:4]:
        copy.start()
    kv_load.start()
    for copy in local[4:]:
        copy.start()

    kept = slots[...] < CAP
    aff = affinity[...]
    weight = route_scale * aff / jnp.sum(aff, 0, keepdims=True) * kept.astype(F32)
    target = jnp.where(kept, ids[...] * CAP + slots[...], -1)
    rows = experts * CAP
    iota = lax.broadcasted_iota(jnp.int32, (rows, tokens), 0)
    dispatch = jnp.zeros((rows, tokens), F32)
    combine = jnp.zeros((rows, tokens), F32)
    for k in range(ids.shape[0]):
        match = target[k : k + 1] == iota
        dispatch = jnp.where(match, 1.0, dispatch)
        combine = jnp.where(match, weight[k : k + 1], combine)
    dispatch = dispatch.astype(BF16)
    combine = combine.T
    high = combine.astype(BF16)
    rest = combine - high.astype(F32)
    mid = rest.astype(BF16)
    low = (rest - mid.astype(F32)).astype(BF16)
    combine3 = jnp.concatenate([high, mid, low], 0)

    local[0].wait()
    for step in range(1, n_tp):
        arrival(hid_all.at[tp_id(step)], hid_rsem.at[tp_id(step)]).wait()
        arrival(gain_all.at[tp_id(step)], gain_rsem.at[tp_id(step)]).wait()
    for g in range(GROUPS):
        span = pl.ds(g * per_group, per_group)
        for step in range(1, n_tp):
            copy = tp_copy(
                cache.at[span], kv_buf.at[span, tp], kv_ssem.at[step, g], kv_rsem.at[tp, g], step
            )
            copy.start()
            sends.append(copy)
    square = jnp.zeros((tokens, 1), F32)
    for b in range(n_tp):
        wide = hid_all[b].astype(F32)
        square = square + jnp.sum(wide * wide, -1, keepdims=True)
    scale = lax.rsqrt(square / d_all + epsilon)
    for b in range(n_tp):
        normed = (hid_all[b].astype(F32) * scale * gain_all[b]).astype(BF16)
        picked = jnp.dot(dispatch, normed, preferred_element_type=F32)
        send[:, b] = picked.reshape(experts, CAP, d_loc).astype(BF16)
    for step in range(1, experts):
        peer = ex_id(step)
        copy = pltpu.make_async_remote_copy(
            src_ref=send.at[peer],
            dst_ref=arrived.at[me],
            send_sem=row_ssem.at[step],
            recv_sem=row_rsem.at[me],
            device_id=ex_dev(peer),
            device_id_type=MESH,
        )
        copy.start()
        sends.append(copy)
    arrived[me] = send[me]

    local[1].wait()
    kv_load.wait()
    heads = queries.shape[1]
    span_len = cache.shape[1]
    total_len = n_tp * span_len

    def attend(g):
        span = pl.ds(g * per_group, per_group)
        for step in range(1, n_tp):
            arrival(kv_buf.at[span, tp_id(step)], kv_rsem.at[tp_id(step), g]).wait()

        def body(i, carry):
            t = g * per_group + i
            block = kv_buf[t].reshape(total_len, kvc)
            scores = (
                lax.dot_general(
                    q_buf[t], block, (((1,), (1,)), ((), ())), preferred_element_type=F32
                )
                * score_scale
            )
            live = lax.broadcasted_iota(jnp.int32, (heads, total_len), 1) < lengths[t]
            scores = jnp.where(live, scores, -1e30)
            peak = jnp.max(scores, -1, keepdims=True)
            prob = jnp.where(live, jnp.exp(scores - peak), 0.0)
            mass = jnp.sum(prob, -1, keepdims=True)
            acc[t] = jnp.dot(prob.astype(BF16), block[:, :lat], preferred_element_type=F32)
            peaks[t] = jnp.broadcast_to(peak, (heads, 128))
            masses[t] = jnp.broadcast_to(mass, (heads, 128))
            return carry

        lax.fori_loop(0, per_group, body, 0)

    for step in range(1, experts):
        arrival(arrived.at[ex_id(step)], row_rsem.at[ex_id(step)]).wait()
    local[2].wait()
    local[3].wait()
    gate = jnp.zeros((rows, wg.shape[1]), F32)
    upper = jnp.zeros((rows, wg.shape[1]), F32)
    for b in range(n_tp):
        block = arrived[:, b].astype(F32).reshape(rows, d_loc).astype(BF16)
        gate = gate + jnp.dot(block, wg[b * d_loc : (b + 1) * d_loc], preferred_element_type=F32)
        upper = upper + jnp.dot(block, wu[b * d_loc : (b + 1) * d_loc], preferred_element_type=F32)
    units = (gate / (1.0 + jnp.exp(-gate)) * upper).astype(BF16)
    local[4].wait()
    width = 512 if d_all % 512 == 0 else 128
    middle = d_all // width // 2 * width
    halves = [(0, middle), (middle, d_all)]
    for h, (first, last) in enumerate(halves):
        for c in range(first, last, width):
            part = jnp.dot(units, wd[:, c : c + width], preferred_element_type=F32)
            ret_send[:, :, c : c + width] = part.reshape(experts, CAP, width).astype(BF16)
        for step in range(1, experts):
            peer = ex_id(step)
            copy = pltpu.make_async_remote_copy(
                src_ref=ret_send.at[peer, :, first:last],
                dst_ref=ret.at[me, :, first:last],
                send_sem=ret_ssem.at[step, h],
                recv_sem=ret_rsem.at[me, h],
                device_id=ex_dev(peer),
                device_id_type=MESH,
            )
            copy.start()
            sends.append(copy)
    ret[me] = ret_send[me]

    for h, (first, last) in enumerate(halves):
        for step in range(1, experts):
            peer = ex_id(step)
            arrival(ret.at[peer, :, first:last], ret_rsem.at[peer, h]).wait()
        for c in range(first, last, width):
            block = ret[:, :, c : c + width].astype(F32).reshape(rows, width).astype(BF16)
            part = jnp.dot(combine3, block, preferred_element_type=F32)
            tsum[:, c : c + width] = part[:tokens] + (
                part[tokens : 2 * tokens] + part[2 * tokens : 3 * tokens]
            )
    for p in range(n_tp):
        rs_send[p] = tsum[:, p * d_loc : (p + 1) * d_loc].astype(BF16)
    for step in range(1, n_tp):
        copy = tp_copy(
            rs_send.at[tp_id(step)], rs_recv.at[tp], rs_ssem.at[step], rs_rsem.at[tp], step
        )
        copy.start()
        sends.append(copy)
    rs_recv[tp] = rs_send[tp]
    for g in range(GROUPS // 2):
        attend(g)
    local[5].wait()
    for step in range(1, n_tp):
        arrival(rs_recv.at[tp_id(step)], rs_rsem.at[tp_id(step)]).wait()
    moe = rs_recv[0].astype(F32)
    for p in range(1, n_tp):
        moe = moe + rs_recv[p].astype(F32)
    next_hidden = (hid_all[tp].astype(F32) + moe).astype(BF16)
    next_out[...] = next_hidden
    next_wide = next_hidden.astype(F32)
    square = jnp.sum(next_wide * next_wide, -1, keepdims=True)
    scaled = (next_wide * attn_gain[...].reshape(1, d_loc)).astype(BF16)
    kvp = up(kvc, 128)
    if kvp > kvc:
        key_send[:, kvp - 128 : kvp] = jnp.zeros((tokens, 128), F32)
    key_send[:, :kvc] = lax.dot_general(
        scaled, wk[...], (((1,), (1,)), ((), ())), preferred_element_type=F32
    )
    key_send[:, kvp : kvp + 128] = jnp.broadcast_to(square, (tokens, 128))
    for step in range(1, n_tp):
        copy = tp_copy(key_send, key_recv.at[tp], key_ssem.at[step], key_rsem.at[tp], step)
        copy.start()
        sends.append(copy)
    key_recv[tp] = key_send[...]
    for g in range(GROUPS // 2, GROUPS):
        attend(g)

    half = (kvc - lat) // 2
    lane = lax.broadcasted_iota(jnp.int32, (tokens, 2 * half), 1)
    pair = jnp.where(lane < half, lane, lane - half).astype(F32)
    freq = jnp.exp(pair * (-9.210340371976184 / half))
    row_id = lax.broadcasted_iota(jnp.int32, (tokens, 2 * half), 0)
    place = jnp.zeros((tokens, 2 * half), F32)
    for t in range(tokens):
        place = jnp.where(row_id == t, lengths[t].astype(F32), place)
    angle = place * freq
    cos_table = jnp.cos(angle)
    sin_table = jnp.where(lane < half, -1.0, 1.0) * jnp.sin(angle)

    for step in range(1, n_tp):
        arrival(key_recv.at[tp_id(step)], key_rsem.at[tp_id(step)]).wait()
    total = key_recv[0]
    for p in range(1, n_tp):
        total = total + key_recv[p]
    down = total * lax.rsqrt(total[:, kvp : kvp + 1] / d_all + epsilon)
    latent = down[:, :lat]
    latent = (
        latent
        * lax.rsqrt(jnp.mean(latent * latent, -1, keepdims=True) + epsilon)
        * kv_gain[...]
    )
    rope = down[:, lat:kvc]
    swapped = jnp.concatenate([rope[:, half:], rope[:, :half]], 1)
    rope = rope * cos_table + swapped * sin_table
    keys[:, :lat] = latent.astype(BF16).astype(F32)
    keys[:, lat:kvc] = rope.astype(BF16).astype(F32)

    def finish(t, carry):
        key = keys[pl.ds(t, 1), :]
        own = jnp.sum(q_buf[t].astype(F32) * key, -1, keepdims=True) * score_scale
        peak = peaks[t][:, :1]
        mass = masses[t][:, :1]
        top = jnp.maximum(peak, own)
        factor = jnp.exp(peak - top)
        own_prob = jnp.exp(own - top)
        inverse = 1.0 / (mass * factor + own_prob)
        own_b = own_prob.astype(BF16).astype(F32)
        latent_out[t] = (acc[t] * (factor * inverse) + (own_b * inverse) * key[:, :lat]).astype(
            BF16
        )
        return carry

    lax.fori_loop(0, tokens, finish, 0)
    for copy in sends:
        copy.wait_send()


def solution(mesh):
    n_tp, n_ep, n_mb = mesh.shape["tp"], mesh.shape["ep"], mesh.shape["mb"]
    experts = n_ep * n_mb

    def local(
        hidden,
        moe_gain,
        expert_ids,
        slots,
        affinity,
        w_gate,
        w_up,
        w_down,
        attn_gain,
        w_dkv,
        kv_gain,
        queries,
        cache,
        lengths,
    ):
        tokens, d_loc = hidden.shape
        d_all = d_loc * n_tp
        heads, kvc = queries.shape[1:]
        span = cache.shape[1]
        lat = kv_gain.shape[0]
        hid_dim = w_gate.shape[2]
        wide = up(kvc, 128) + 128
        any_space = pl.BlockSpec(memory_space=pl.ANY)
        vmem = pl.BlockSpec(memory_space=pltpu.VMEM)
        smem = pl.BlockSpec(memory_space=pltpu.SMEM)
        dma = pltpu.SemaphoreType.DMA
        return pl.pallas_call(
            functools.partial(kernel, n_tp, n_ep, n_mb),
            out_shape=(
                jax.ShapeDtypeStruct((tokens, d_loc), BF16),
                jax.ShapeDtypeStruct((tokens, heads, lat), BF16),
            ),
            in_specs=[
                any_space,
                vmem,
                vmem,
                vmem,
                vmem,
                any_space,
                any_space,
                any_space,
                vmem,
                any_space,
                vmem,
                any_space,
                any_space,
                smem,
            ],
            out_specs=(vmem, vmem),
            scratch_shapes=[
                pltpu.VMEM((n_tp, tokens, d_loc), BF16),
                pltpu.VMEM((n_tp, 1, d_loc), F32),
                pltpu.VMEM((experts, n_tp, CAP, d_loc), BF16),
                pltpu.VMEM((experts, n_tp, CAP, d_loc), BF16),
                pltpu.VMEM((d_all, hid_dim), BF16),
                pltpu.VMEM((d_all, hid_dim), BF16),
                pltpu.VMEM((hid_dim, d_all), BF16),
                pltpu.VMEM((kvc, d_loc), BF16),
                pltpu.VMEM((experts, CAP, d_all), BF16),
                pltpu.VMEM((experts, CAP, d_all), BF16),
                pltpu.VMEM((tokens, d_all), F32),
                pltpu.VMEM((n_tp, tokens, d_loc), BF16),
                pltpu.VMEM((n_tp, tokens, d_loc), BF16),
                pltpu.VMEM((tokens, wide), F32),
                pltpu.VMEM((n_tp, tokens, wide), F32),
                pltpu.VMEM((tokens, heads, kvc), BF16),
                pltpu.VMEM((tokens, n_tp, span, kvc), BF16),
                pltpu.VMEM((tokens, heads, lat), F32),
                pltpu.VMEM((tokens, heads, 128), F32),
                pltpu.VMEM((tokens, heads, 128), F32),
                pltpu.VMEM((tokens, kvc), F32),
                dma((6,)),
                dma,
                dma((n_tp,)),
                dma((n_tp,)),
                dma((n_tp,)),
                dma((n_tp,)),
                dma((n_tp, GROUPS)),
                dma((n_tp, GROUPS)),
                dma((experts,)),
                dma((experts,)),
                dma((experts, 2)),
                dma((experts, 2)),
                dma((n_tp,)),
                dma((n_tp,)),
                dma((n_tp,)),
                dma((n_tp,)),
            ],
            compiler_params=pltpu.CompilerParams(
                collective_id=0, has_side_effects=True, vmem_limit_bytes=60 * 1024 * 1024
            ),
        )(
            hidden,
            moe_gain,
            expert_ids.T,
            slots.T,
            affinity.T,
            w_gate,
            w_up,
            w_down,
            attn_gain,
            w_dkv.T,
            kv_gain[None],
            queries,
            cache,
            lengths,
        )

    return jax.shard_map(
        local,
        mesh=mesh,
        in_specs=(
            P(("grp", "ep", "mb"), "tp"),
            P("tp"),
            P(("grp", "ep", "mb"), None),
            P(("grp", "ep", "mb"), None),
            P(("grp", "ep", "mb"), None),
            P(("ep", "mb"), None, "tp"),
            P(("ep", "mb"), None, "tp"),
            P(("ep", "mb"), "tp", None),
            P("tp"),
            P("tp", None),
            P(),
            P(("grp", "ep", "mb"), "tp", None),
            P(("grp", "ep", "mb"), "tp", None),
            P(("grp", "ep", "mb")),
        ),
        out_specs=(P(("grp", "ep", "mb"), "tp"), P(("grp", "ep", "mb"), "tp", None)),
        check_vma=False,
    )
```

```python
import functools

import jax
import jax.numpy as jnp
from jax import lax
from jax.experimental import pallas as pl
from jax.experimental.pallas import tpu as pltpu
from jax.sharding import PartitionSpec as P

CAP = 8
GROUPS = 4
epsilon = 1e-06
route_scale = 2.5
score_scale = 192.0 ** (-0.5)
MESH = pl.DeviceIdType.MESH
F32 = jnp.float32
BF16 = jnp.bfloat16


def up(value, step):
    return -(-value // step) * step


def kernel(
    n_tp,
    n_ep,
    n_mb,
    hidden,
    moe_gain,
    ids,
    slots,
    affinity,
    w_gate,
    w_up,
    w_down,
    attn_gain,
    w_dkv,
    kv_gain,
    queries,
    cache,
    lengths,
    next_out,
    latent_out,
    hid_all,
    gain_all,
    send,
    arrived,
    wg,
    wu,
    wd,
    wk,
    ret_send,
    ret,
    tsum,
    rs_send,
    rs_recv,
    key_send,
    key_recv,
    q_buf,
    kv_buf,
    acc,
    peaks,
    masses,
    keys,
    load_sem,
    kv_load_sem,
    hid_ssem,
    hid_rsem,
    gain_ssem,
    gain_rsem,
    kv_ssem,
    kv_rsem,
    row_ssem,
    row_rsem,
    ret_ssem,
    ret_rsem,
    rs_ssem,
    rs_rsem,
    key_ssem,
    key_rsem,
):
    experts = n_ep * n_mb
    tokens, d_loc = hidden.shape
    d_all = d_loc * n_tp
    lat = kv_gain.shape[1]
    kvc = cache.shape[2]
    per_group = tokens // GROUPS
    tp = lax.axis_index("tp")
    me = lax.axis_index("ep") * n_mb + lax.axis_index("mb")

    def tp_id(step):
        return lax.rem(tp + step, n_tp)

    def ex_id(step):
        return lax.rem(me + step, experts)

    def ex_dev(index):
        return {"ep": index // n_mb, "mb": lax.rem(index, n_mb)}

    local = [
        pltpu.make_async_copy(hidden, hid_all.at[tp], load_sem.at[0]),
        pltpu.make_async_copy(queries, q_buf, load_sem.at[1]),
        pltpu.make_async_copy(w_gate.at[0], wg, load_sem.at[2]),
        pltpu.make_async_copy(w_up.at[0], wu, load_sem.at[3]),
        pltpu.make_async_copy(w_down.at[0], wd, load_sem.at[4]),
        pltpu.make_async_copy(w_dkv, wk, load_sem.at[5]),
    ]
    kv_load = pltpu.make_async_copy(cache, kv_buf.at[:, tp], kv_load_sem)
    local[0].start()
    gain_all[tp] = moe_gain[...].reshape(1, d_loc)

    barrier = pltpu.get_barrier_semaphore()
    for step in range(1, n_tp):
        pl.semaphore_signal(barrier, inc=1, device_id={"tp": tp_id(step)}, device_id_type=MESH)
    for step in range(1, experts):
        pl.semaphore_signal(barrier, inc=1, device_id=ex_dev(ex_id(step)), device_id_type=MESH)
    kept = slots[...] < CAP
    aff = affinity[...]
    weight = route_scale * aff / jnp.sum(aff, 0, keepdims=True) * kept.astype(F32)
    target = jnp.where(kept, ids[...] * CAP + slots[...], -1)
    rows = experts * CAP
    iota = lax.broadcasted_iota(jnp.int32, (rows, tokens), 0)
    dispatch = jnp.zeros((rows, tokens), F32)
    combine = jnp.zeros((rows, tokens), F32)
    for k in range(ids.shape[0]):
        match = target[k : k + 1] == iota
        dispatch = jnp.where(match, 1.0, dispatch)
        combine = jnp.where(match, weight[k : k + 1], combine)
    dispatch = dispatch.astype(BF16)
    combine = combine.T
    high = combine.astype(BF16)
    rest = combine - high.astype(F32)
    mid = rest.astype(BF16)
    low = (rest - mid.astype(F32)).astype(BF16)
    combine3 = jnp.concatenate([high, mid, low], 0)

    def pick(block):
        picked = jnp.dot(dispatch, hid_all[block], preferred_element_type=F32)
        send[:, block] = picked.reshape(experts, CAP, d_loc).astype(BF16)

    def ship(block, turn):
        for step in range(1, experts):
            peer = ex_id(step)
            copy = pltpu.make_async_remote_copy(
                src_ref=send.at[peer, block],
                dst_ref=arrived.at[me, block],
                send_sem=row_ssem.at[step, turn],
                recv_sem=row_rsem.at[me, block],
                device_id=ex_dev(peer),
                device_id_type=MESH,
            )
            copy.start()
            sends.append(copy)
        arrived[me, block] = send[me, block]

    local[0].wait()
    pick(tp)
    pl.semaphore_wait(barrier, n_tp - 1 + experts - 1)

    def tp_copy(src, dst, ssem, rsem, step):
        return pltpu.make_async_remote_copy(
            src_ref=src,
            dst_ref=dst,
            send_sem=ssem,
            recv_sem=rsem,
            device_id={"tp": tp_id(step)},
            device_id_type=MESH,
        )

    def arrival(dst, rsem):
        return pltpu.make_async_copy(dst, dst, rsem)

    sends = []
    for step in range(1, n_tp):
        for src, dst, ssem, rsem in (
            (hidden, hid_all, hid_ssem, hid_rsem),
            (gain_all.at[tp], gain_all, gain_ssem, gain_rsem),
        ):
            copy = tp_copy(src, dst.at[tp], ssem.at[step], rsem.at[tp], step)
            copy.start()
            sends.append(copy)
    ship(tp, 0)
    for g in range(GROUPS):
        span = pl.ds(g * per_group, per_group)
        for step in range(1, n_tp):
            copy = tp_copy(
                cache.at[span], kv_buf.at[span, tp], kv_ssem.at[step, g], kv_rsem.at[tp, g], step
            )
            copy.start()
            sends.append(copy)
    for copy in local[1:4]:
        copy.start()
    kv_load.start()
    for copy in local[4:]:
        copy.start()

    for step in range(1, n_tp):
        arrival(hid_all.at[tp_id(step)], hid_rsem.at[tp_id(step)]).wait()
        arrival(gain_all.at[tp_id(step)], gain_rsem.at[tp_id(step)]).wait()
    for turn in range(1, n_tp):
        pick(tp_id(turn))
        ship(tp_id(turn), turn)

    local[1].wait()
    kv_load.wait()
    heads = queries.shape[1]
    span_len = cache.shape[1]
    total_len = n_tp * span_len

    def attend(g):
        span = pl.ds(g * per_group, per_group)
        for step in range(1, n_tp):
            arrival(kv_buf.at[span, tp_id(step)], kv_rsem.at[tp_id(step), g]).wait()

        def body(i, carry):
            t = g * per_group + i
            block = kv_buf[t].reshape(total_len, kvc)
            scores = (
                lax.dot_general(
                    q_buf[t], block, (((1,), (1,)), ((), ())), preferred_element_type=F32
                )
                * score_scale
            )
            live = lax.broadcasted_iota(jnp.int32, (heads, total_len), 1) < lengths[t]
            scores = jnp.where(live, scores, -1e30)
            peak = jnp.max(scores, -1, keepdims=True)
            prob = jnp.where(live, jnp.exp(scores - peak), 0.0)
            mass = jnp.sum(prob, -1, keepdims=True)
            acc[t] = jnp.dot(prob.astype(BF16), block[:, :lat], preferred_element_type=F32)
            peaks[t] = jnp.broadcast_to(peak, (heads, 128))
            masses[t] = jnp.broadcast_to(mass, (heads, 128))
            return carry

        lax.fori_loop(0, per_group, body, 0)

    local[2].wait()
    local[3].wait()
    gate = jnp.zeros((rows, wg.shape[1]), F32)
    upper = jnp.zeros((rows, wg.shape[1]), F32)
    square = jnp.zeros((rows, 1), F32)
    for turn in range(n_tp):
        b = tp_id(turn)
        for step in range(1, experts):
            peer = ex_id(step)
            arrival(arrived.at[peer, b], row_rsem.at[peer, b]).wait()
        wide = arrived[:, b].astype(F32).reshape(rows, d_loc)
        square = square + jnp.sum(wide * wide, -1, keepdims=True)
        block = (wide * gain_all[b]).astype(BF16)
        deep = pl.ds(pl.multiple_of(b * d_loc, d_loc & -d_loc), d_loc)
        gate = gate + jnp.dot(block, wg[deep], preferred_element_type=F32)
        upper = upper + jnp.dot(block, wu[deep], preferred_element_type=F32)
    scale = lax.rsqrt(square / d_all + epsilon)
    gate = gate * scale
    upper = upper * scale
    units = (gate / (1.0 + jnp.exp(-gate)) * upper).astype(BF16)
    local[4].wait()
    width = 512 if d_all % 512 == 0 else 128
    aligned = d_loc % 128 == 0
    if aligned:
        width = next(w for w in (896, 512, 384, 256, 128) if d_loc % w == 0)
        pieces = [
            (pl.multiple_of(tp_id(turn) * d_loc, 128), d_loc) for turn in (*range(1, n_tp), 0)
        ]
    else:
        middle = d_all // width // 2 * width
        pieces = [(0, middle), (middle, d_all - middle)]

    def columns(start, size):
        return pl.ds(pl.multiple_of(start, 128), size)

    for h, (first, size) in enumerate(pieces):
        for c in range(0, size, width):
            part = jnp.dot(units, wd[:, columns(first + c, width)], preferred_element_type=F32)
            ret_send[:, :, columns(first + c, width)] = part.reshape(
                experts, CAP, width
            ).astype(BF16)
        for step in range(1, experts):
            peer = ex_id(step)
            copy = pltpu.make_async_remote_copy(
                src_ref=ret_send.at[peer, :, columns(first, size)],
                dst_ref=ret.at[me, :, columns(first, size)],
                send_sem=ret_ssem.at[step, h],
                recv_sem=ret_rsem.at[me, h],
                device_id=ex_dev(peer),
                device_id_type=MESH,
            )
            copy.start()
            sends.append(copy)
    ret[me] = ret_send[me]

    def exchange(step):
        copy = tp_copy(
            rs_send.at[tp_id(step)], rs_recv.at[tp], rs_ssem.at[step], rs_rsem.at[tp], step
        )
        copy.start()
        sends.append(copy)

    for h, (first, size) in enumerate(pieces):
        for step in range(1, experts):
            peer = ex_id(step)
            arrival(ret.at[peer, :, columns(first, size)], ret_rsem.at[peer, h]).wait()
        for c in range(0, size, width):
            block = ret[:, :, columns(first + c, width)].astype(F32)
            block = block.reshape(rows, width).astype(BF16)
            part = jnp.dot(combine3, block, preferred_element_type=F32)
            part = part[:tokens] + (part[tokens : 2 * tokens] + part[2 * tokens : 3 * tokens])
            if aligned:
                rs_send[tp_id(h + 1), :, c : c + width] = part.astype(BF16)
            else:
                tsum[:, columns(first + c, width)] = part
        if aligned and h < n_tp - 1:
            exchange(h + 1)
        if h == 0:
            for g in range(GROUPS // 2):
                attend(g)
    if not aligned:
        for p in range(n_tp):
            rs_send[p] = tsum[:, p * d_loc : (p + 1) * d_loc].astype(BF16)
        for step in range(1, n_tp):
            exchange(step)
    rs_recv[tp] = rs_send[tp]
    local[5].wait()
    for step in range(1, n_tp):
        arrival(rs_recv.at[tp_id(step)], rs_rsem.at[tp_id(step)]).wait()
    moe = rs_recv[0].astype(F32)
    for p in range(1, n_tp):
        moe = moe + rs_recv[p].astype(F32)
    next_hidden = (hid_all[tp].astype(F32) + moe).astype(BF16)
    next_out[...] = next_hidden
    next_wide = next_hidden.astype(F32)
    square = jnp.sum(next_wide * next_wide, -1, keepdims=True)
    scaled = (next_wide * attn_gain[...].reshape(1, d_loc)).astype(BF16)
    kvp = up(kvc, 128)
    if kvp > kvc:
        key_send[:, kvp - 128 : kvp] = jnp.zeros((tokens, 128), F32)
    key_send[:, :kvc] = lax.dot_general(
        scaled, wk[...], (((1,), (1,)), ((), ())), preferred_element_type=F32
    )
    key_send[:, kvp : kvp + 128] = jnp.broadcast_to(square, (tokens, 128))
    for step in range(1, n_tp):
        copy = tp_copy(key_send, key_recv.at[tp], key_ssem.at[step], key_rsem.at[tp], step)
        copy.start()
        sends.append(copy)
    key_recv[tp] = key_send[...]
    for g in range(GROUPS // 2, GROUPS):
        attend(g)

    half = (kvc - lat) // 2
    lane = lax.broadcasted_iota(jnp.int32, (tokens, 2 * half), 1)
    pair = jnp.where(lane < half, lane, lane - half).astype(F32)
    freq = jnp.exp(pair * (-9.210340371976184 / half))
    row_id = lax.broadcasted_iota(jnp.int32, (tokens, 2 * half), 0)
    place = jnp.zeros((tokens, 2 * half), F32)
    for t in range(tokens):
        place = jnp.where(row_id == t, lengths[t].astype(F32), place)
    angle = place * freq
    cos_table = jnp.cos(angle)
    sin_table = jnp.where(lane < half, -1.0, 1.0) * jnp.sin(angle)

    for step in range(1, n_tp):
        arrival(key_recv.at[tp_id(step)], key_rsem.at[tp_id(step)]).wait()
    total = key_recv[0]
    for p in range(1, n_tp):
        total = total + key_recv[p]
    down = total * lax.rsqrt(total[:, kvp : kvp + 1] / d_all + epsilon)
    latent = down[:, :lat]
    latent = (
        latent
        * lax.rsqrt(jnp.mean(latent * latent, -1, keepdims=True) + epsilon)
        * kv_gain[...]
    )
    rope = down[:, lat:kvc]
    swapped = jnp.concatenate([rope[:, half:], rope[:, :half]], 1)
    rope = rope * cos_table + swapped * sin_table
    keys[:, :lat] = latent.astype(BF16).astype(F32)
    keys[:, lat:kvc] = rope.astype(BF16).astype(F32)

    def finish(t, carry):
        key = keys[pl.ds(t, 1), :]
        own = jnp.sum(q_buf[t].astype(F32) * key, -1, keepdims=True) * score_scale
        peak = peaks[t][:, :1]
        mass = masses[t][:, :1]
        top = jnp.maximum(peak, own)
        factor = jnp.exp(peak - top)
        own_prob = jnp.exp(own - top)
        inverse = 1.0 / (mass * factor + own_prob)
        own_b = own_prob.astype(BF16).astype(F32)
        latent_out[t] = (acc[t] * (factor * inverse) + (own_b * inverse) * key[:, :lat]).astype(
            BF16
        )
        return carry

    lax.fori_loop(0, tokens, finish, 0)
    for copy in sends:
        copy.wait_send()


def solution(mesh):
    n_tp, n_ep, n_mb = mesh.shape["tp"], mesh.shape["ep"], mesh.shape["mb"]
    experts = n_ep * n_mb

    def local(
        hidden,
        moe_gain,
        expert_ids,
        slots,
        affinity,
        w_gate,
        w_up,
        w_down,
        attn_gain,
        w_dkv,
        kv_gain,
        queries,
        cache,
        lengths,
    ):
        tokens, d_loc = hidden.shape
        d_all = d_loc * n_tp
        heads, kvc = queries.shape[1:]
        span = cache.shape[1]
        lat = kv_gain.shape[0]
        hid_dim = w_gate.shape[2]
        wide = up(kvc, 128) + 128
        any_space = pl.BlockSpec(memory_space=pl.ANY)
        vmem = pl.BlockSpec(memory_space=pltpu.VMEM)
        smem = pl.BlockSpec(memory_space=pltpu.SMEM)
        dma = pltpu.SemaphoreType.DMA
        return pl.pallas_call(
            functools.partial(kernel, n_tp, n_ep, n_mb),
            out_shape=(
                jax.ShapeDtypeStruct((tokens, d_loc), BF16),
                jax.ShapeDtypeStruct((tokens, heads, lat), BF16),
            ),
            in_specs=[
                any_space,
                vmem,
                vmem,
                vmem,
                vmem,
                any_space,
                any_space,
                any_space,
                vmem,
                any_space,
                vmem,
                any_space,
                any_space,
                smem,
            ],
            out_specs=(vmem, vmem),
            scratch_shapes=[
                pltpu.VMEM((n_tp, tokens, d_loc), BF16),
                pltpu.VMEM((n_tp, 1, d_loc), F32),
                pltpu.VMEM((experts, n_tp, CAP, d_loc), BF16),
                pltpu.VMEM((experts, n_tp, CAP, d_loc), BF16),
                pltpu.VMEM((d_all, hid_dim), BF16),
                pltpu.VMEM((d_all, hid_dim), BF16),
                pltpu.VMEM((hid_dim, d_all), BF16),
                pltpu.VMEM((kvc, d_loc), BF16),
                pltpu.VMEM((experts, CAP, d_all), BF16),
                pltpu.VMEM((experts, CAP, d_all), BF16),
                pltpu.VMEM((tokens, d_all), F32),
                pltpu.VMEM((n_tp, tokens, d_loc), BF16),
                pltpu.VMEM((n_tp, tokens, d_loc), BF16),
                pltpu.VMEM((tokens, wide), F32),
                pltpu.VMEM((n_tp, tokens, wide), F32),
                pltpu.VMEM((tokens, heads, kvc), BF16),
                pltpu.VMEM((tokens, n_tp, span, kvc), BF16),
                pltpu.VMEM((tokens, heads, lat), F32),
                pltpu.VMEM((tokens, heads, 128), F32),
                pltpu.VMEM((tokens, heads, 128), F32),
                pltpu.VMEM((tokens, kvc), F32),
                dma((6,)),
                dma,
                dma((n_tp,)),
                dma((n_tp,)),
                dma((n_tp,)),
                dma((n_tp,)),
                dma((n_tp, GROUPS)),
                dma((n_tp, GROUPS)),
                dma((experts, n_tp)),
                dma((experts, n_tp)),
                dma((experts, max(2, n_tp))),
                dma((experts, max(2, n_tp))),
                dma((n_tp,)),
                dma((n_tp,)),
                dma((n_tp,)),
                dma((n_tp,)),
            ],
            compiler_params=pltpu.CompilerParams(
                collective_id=0, has_side_effects=True, vmem_limit_bytes=60 * 1024 * 1024
            ),
        )(
            hidden,
            moe_gain,
            expert_ids.T,
            slots.T,
            affinity.T,
            w_gate,
            w_up,
            w_down,
            attn_gain,
            w_dkv.T,
            kv_gain[None],
            queries,
            cache,
            lengths,
        )

    return jax.shard_map(
        local,
        mesh=mesh,
        in_specs=(
            P(("grp", "ep", "mb"), "tp"),
            P("tp"),
            P(("grp", "ep", "mb"), None),
            P(("grp", "ep", "mb"), None),
            P(("grp", "ep", "mb"), None),
            P(("ep", "mb"), None, "tp"),
            P(("ep", "mb"), None, "tp"),
            P(("ep", "mb"), "tp", None),
            P("tp"),
            P("tp", None),
            P(),
            P(("grp", "ep", "mb"), "tp", None),
            P(("grp", "ep", "mb"), "tp", None),
            P(("grp", "ep", "mb")),
        ),
        out_specs=(P(("grp", "ep", "mb"), "tp"), P(("grp", "ep", "mb"), "tp", None)),
        check_vma=False,
    )
```
